32 devices in a mesh: grp: 2 (over x), row: 16 (over z, y, core).
Axes of the slice: x: 2, y: 2, z: 4, core: 2. Of those that a mesh axis runs over, the one named last changes fastest.
Arguments:
- pair_map: bfloat16 [256, 128, 128], P(('grp', 'row')), parts along dimension 0, may hold values from -6 to 6
- norm_gain: float32 [128], replicated, may hold values from 0.1 to 1.9
- w_query: bfloat16 [128, 128], replicated, may hold values from -30 to 30
- w_key: bfloat16 [128, 128], replicated, may hold values from -1 to 1
- w_value: bfloat16 [128, 128], replicated, may hold values from -0.5 to 0.5
- w_gate: bfloat16 [128, 128], replicated, may hold values from -0.5 to 0.5
- w_bias: bfloat16 [128, 4], replicated, may hold values from -12 to 12
- w_output: bfloat16 [128, 128], replicated, may hold values from -0.5 to 0.5
- window_start: int32 [256], P(('grp', 'row')), parts along dimension 0, may hold values from 0 to 63
- key_length: int32 [256], P(('grp', 'row')), parts along dimension 0, may hold values from 32 to 64
Outputs:
- update: bfloat16 [256, 128, 128], P('grp', 'row'), parts along dimension 0
The draws below stay inside these ranges and needn't reach their ends.
There are 2 independent parts, one for each index of `grp`. The reference program is written for one: setup_inputs(seed, part) draws one part's arguments, and reference() takes and returns one part's arrays. A program takes and returns all parts, laid end to end along the dimension named above; an argument that names none is the same for every part. Nothing has to cross between parts.
All inputs are finite; a program needn't handle non-finite values.
Results may differ from the reference program's by a relative error of at most 0.0025.
The reference program's roundings to bfloat16 on the way (of `normed`, `weights` and `gated`) count: a program that leaves them out, or rounds other values in their place, can miss the bound.
Values may be sent and summed in bfloat16 or wider, within the bound.
A program may use at most 128 MiB of HBM per device.

```python
import jax
import jax.numpy as jnp
from jax import lax

C = 128
H = 4
DH = 32
N = 128


def paired_base(key):
    base = jax.random.fold_in(key, 4111)
    scale = C ** (-0.5)
    shared = jnp.clip(jax.random.normal(jax.random.fold_in(base, 1), (C, C), jnp.float32), -3.0, 3.0) * scale
    return (base, shared)


def draw_w_key(key, part):
    base, shared = paired_base(key)
    return shared.astype(jnp.bfloat16)


def draw_w_query(key, part):
    base, shared = paired_base(key)
    scale = C ** (-0.5)
    noise = jnp.clip(jax.random.normal(jax.random.fold_in(base, 2), (C, C), jnp.float32), -3.0, 3.0) * scale
    result = noise
    return jnp.clip(result, -30.0, 30.0).astype(jnp.bfloat16)


def draw_w_bias(key, part):
    base, shared = paired_base(key)
    scale = C ** (-0.5)
    raw = jnp.clip(jax.random.normal(jax.random.fold_in(base, 5), (C, H), jnp.float32), -3.0, 3.0) * scale
    result = raw * 1.5
    return jnp.clip(result, -12.0, 12.0).astype(jnp.bfloat16)


def place_ends(entries, own_key, least, top_value):
    longest = entries.shape.index(max(entries.shape))
    spots = []
    for shift in (0, 1):
        where = [jax.random.randint(jax.random.fold_in(own_key, axis), (), 0, length) for axis, length in enumerate(entries.shape)]
        where[longest] = (where[longest] + shift) % entries.shape[longest]
        spots.append(tuple(where))
    return entries.at[spots[0]].set(least).at[spots[1]].set(top_value)


def levels(stream_key, dims, pieces, smallest, high):
    factor_of, own = 1.0, jax.random.fold_in(stream_key, 6)
    for axis_at, parts in pieces:
        heights = jnp.exp(jax.random.uniform(jax.random.fold_in(own, axis_at), (parts,), jnp.float32, smallest / len(pieces), high / len(pieces)))
        factor_of = factor_of * jnp.repeat(heights, dims[axis_at] // parts).reshape([-1 if axis == axis_at else 1 for axis in range(len(dims))])
    return factor_of


def normal_values(stream_key, dims, scale, reach, split=(), kind=jnp.bfloat16):
    values = jax.random.normal(stream_key, dims, jnp.float32) * scale
    if len(split) > 0:
        values = levels(stream_key, dims, split, -0.22, 0.18) * values
    return jnp.clip(values, min=-reach, max=reach).astype(kind)


def setup_inputs(seed: int = 0, part: int = 0) -> dict:
    keys = jax.random.split(jax.random.key(seed), 11)
    part_keys = jax.random.split(jax.random.fold_in(keys[10], part), 11)
    return {
        "pair_map": normal_values(part_keys[0], (N, N, C), 1.0, 6.0, ((0, 16),)),
        "norm_gain": jnp.clip(1.0 + 0.18 * jax.random.normal(keys[1], (C,), jnp.float32), 0.1, 1.9),
        "w_query": draw_w_query(jax.random.fold_in(keys[10], 71), part),
        "w_key": draw_w_key(jax.random.fold_in(keys[10], 71), part),
        "w_value": normal_values(keys[4], (C, C), C ** -0.5, 0.5),
        "w_gate": normal_values(keys[5], (C, C), C ** -0.5, 0.5),
        "w_bias": draw_w_bias(jax.random.fold_in(keys[10], 71), part),
        "w_output": normal_values(keys[7], (C, C), C ** -0.5, 0.5),
        "window_start": place_ends(jax.random.randint(part_keys[8], (N,), 0, N // 2), jax.random.fold_in(part_keys[8], 1), 0, (N // 2) - 1).astype(jnp.int32),
        "key_length": place_ends(jax.random.randint(part_keys[9], (N,), N // 4, N // 2 + 1), jax.random.fold_in(part_keys[9], 1), N // 4, (N // 2 + 1) - 1).astype(jnp.int32),
    }


def normalize(rows, norm_gain):
    values = rows.astype(jnp.float32)
    center = lax.optimization_barrier(jnp.mean(values, axis=-1, keepdims=True))
    spread = lax.optimization_barrier(jnp.mean((values - center) ** 2, axis=-1, keepdims=True))
    return ((values - center) * lax.rsqrt(spread + 1e-05) * norm_gain).astype(jnp.bfloat16)

def reference(pair_map, norm_gain, w_query, w_key, w_value, w_gate, w_bias, w_output, window_start, key_length):
    positions = jnp.arange(N, dtype=jnp.int32)

    def bias_row(row_data):
        normed = normalize(row_data, norm_gain)
        return jnp.dot(normed, w_bias, preferred_element_type=jnp.float32)
    bias = lax.map(bias_row, pair_map)
    bias = jnp.transpose(bias, (2, 0, 1)).astype(jnp.float32)

    def one_row(inputs):
        row_data, first, count = inputs
        normed = normalize(row_data, norm_gain)
        query = jnp.dot(normed, w_query, preferred_element_type=jnp.float32).astype(jnp.bfloat16)
        key = jnp.dot(normed, w_key, preferred_element_type=jnp.float32).astype(jnp.bfloat16)
        value = jnp.dot(normed, w_value, preferred_element_type=jnp.float32).astype(jnp.bfloat16)
        gate = jnp.dot(normed, w_gate, preferred_element_type=jnp.float32).astype(jnp.bfloat16)
        query = query.astype(jnp.float32).reshape(N, H, DH)
        key = key.astype(jnp.float32).reshape(N, H, DH)
        value = value.astype(jnp.float32).reshape(N, H, DH)
        scores = jnp.einsum('jhd,khd->hjk', query, key) * (1.0 / DH ** 0.5) + bias
        valid = (positions >= first) & (positions < first + count)
        scores = jnp.where(valid[None, None, :], scores, jnp.float32(-1e+30))
        top = lax.optimization_barrier(jnp.max(scores, axis=-1, keepdims=True))
        raised = jnp.exp(scores - top)
        weights = (raised / lax.optimization_barrier(jnp.sum(raised, axis=-1, keepdims=True))).astype(jnp.bfloat16)
        attended = jnp.einsum('hjk,khd->jhd', weights.astype(jnp.float32), value).reshape(N, C)
        gated = (jax.nn.sigmoid(gate.astype(jnp.float32)) * attended).astype(jnp.bfloat16)
        return jnp.dot(gated, w_output, preferred_element_type=jnp.float32).astype(jnp.bfloat16)
    return lax.map(one_row, (pair_map, window_start, key_length))
```

```python
import functools
import math

import jax
import jax.numpy as jnp
from jax import lax
from jax.experimental import pallas as pl
from jax.experimental.pallas import tpu as pltpu
from jax.sharding import PartitionSpec as P

H = 4
LOG2E = math.log2(math.e)
MESH = pl.DeviceIdType.MESH
NT = (((1,), (1,)), ((), ()))


def other(index, step, count):
    if count & (count - 1):
        return lax.rem(index + step, count)
    result, bit = 0, 1
    while bit < count:
        a, b = index // bit % 2, step // bit % 2
        result = result + (a + b - 2 * a * b) * bit
        bit *= 2
    return result


def kernel(
    n,
    x_hbm,
    gain_hbm,
    wq_hbm,
    wk_hbm,
    wv_hbm,
    wg_hbm,
    wb_hbm,
    wo_hbm,
    start_ref,
    length_ref,
    out_ref,
    x_ref,
    gain_ref,
    wq_ref,
    wk_ref,
    wv_ref,
    wg_ref,
    wb_ref,
    wo_ref,
    wide_ref,
    bias_ref,
    score_ref,
    value_ref,
    sig_ref,
    gated_ref,
    send_ref,
    in_sem,
    bias_send,
    bias_recv,
    out_send,
    out_recv,
    own_sem,
):
    rows, width, channels = x_ref.shape
    head = channels // H
    chips = n // 2
    me = lax.axis_index("row")
    core, chip = me % 2, me // 2
    mate = me + 1 - 2 * core

    barrier = pltpu.get_barrier_semaphore()

    def greet(step, carry):
        pl.semaphore_signal(
            barrier, inc=1, device_id={"row": lax.rem(me + step, n)}, device_id_type=MESH
        )
        return carry

    lax.fori_loop(1, n, greet, 0)

    loads = [
        pltpu.make_async_copy(source, target, in_sem.at[at])
        for at, (source, target) in enumerate(
            (
                (x_hbm, x_ref),
                (gain_hbm, gain_ref),
                (wb_hbm, wb_ref),
                (wq_hbm, wq_ref),
                (wk_hbm, wk_ref),
                (wv_hbm, wv_ref),
                (wg_hbm, wg_ref),
                (wo_hbm, wo_ref),
            )
        )
    ]
    for load in loads:
        load.start()

    wide_ref[...] = jnp.zeros_like(wide_ref)
    loads[2].wait()
    wide_ref[:, :H] = wb_ref[...].astype(jnp.float32)
    bias_weight = wide_ref[...].T[:8].astype(jnp.bfloat16)
    loads[0].wait()
    loads[1].wait()
    gain = gain_ref[...]
    normed = []
    for i in range(rows):
        values = x_ref[i].astype(jnp.float32)
        center = jnp.mean(values, axis=-1, keepdims=True)
        values = values - center
        spread = jnp.mean(values * values, axis=-1, keepdims=True)
        row = (values * lax.rsqrt(spread + 1e-05) * gain).astype(jnp.bfloat16)
        x_ref[i] = row
        local = lax.dot_general(bias_weight, row, NT, preferred_element_type=jnp.float32)
        local = local * LOG2E
        for h in range(H):
            bias_ref[me, h, i : i + 1, :] = local[h : h + 1]

    pl.semaphore_wait(barrier, n - 1)

    def bias_copy(source, target, slot):
        return pltpu.make_async_remote_copy(
            src_ref=bias_ref.at[source],
            dst_ref=bias_ref.at[source],
            send_sem=bias_send.at[slot],
            recv_sem=bias_recv.at[source],
            device_id={"row": target},
            device_id_type=MESH,
        )

    def send_bias(at, carry):
        peer = other(chip, chips - 1 - at, chips) * 2
        for c in range(2):
            bias_copy(me, peer + c, peer + c).start()
        return carry

    lax.fori_loop(0, chips - 1, send_bias, 0)
    bias_copy(me, mate, mate).start()

    for load in loads[3:7]:
        load.wait()
    lane = lax.broadcasted_iota(jnp.int32, (1, channels), 1) // head
    masks = [(lane == h).astype(jnp.float32).astype(jnp.bfloat16) for h in range(H)]
    place = lax.broadcasted_iota(jnp.int32, (1, width), 1)
    factor = LOG2E / head**0.5

    def project(i):
        row = x_ref[i]

        def through(weight):
            return jnp.dot(row, weight[...], preferred_element_type=jnp.float32)

        query = through(wq_ref).astype(jnp.bfloat16)
        key = through(wk_ref).astype(jnp.bfloat16)
        value = through(wv_ref).astype(jnp.bfloat16)
        gate = through(wg_ref).astype(jnp.bfloat16).astype(jnp.float32)
        sig_ref[i] = jax.nn.sigmoid(gate)
        first = start_ref[i]
        valid = (place >= first) & (place < first + length_ref[i])
        for h in range(H):
            span = slice(h * width, (h + 1) * width)
            value_ref[i, span, :] = value * masks[h]
            part = lax.dot_general(
                query, key * masks[h], NT, preferred_element_type=jnp.float32
            )
            score_ref[i, :, span] = jnp.where(valid, part * factor, jnp.float32(-1e30))

    if width <= 128:
        for i in range(rows):
            project(i)
    else:
        pl.loop(0, rows)(project)
    loads[7].wait()

    both = 2 * rows

    def attend(first):
        columns = pl.ds(pl.multiple_of(first * rows, both), both)
        biases = [bias_ref[pl.ds(first, 2), h].reshape(both, width) for h in range(H)]
        for i in range(rows):
            parts = []
            for h in range(H):
                t = score_ref[i, columns, h * width : (h + 1) * width] + biases[h]
                raised = jnp.exp2(t - jnp.max(t, axis=-1, keepdims=True))
                total = jnp.sum(raised, axis=-1, keepdims=True)
                parts.append((raised * (1.0 / total)).astype(jnp.bfloat16))
            attended = jnp.dot(
                jnp.concatenate(parts, axis=1), value_ref[i], preferred_element_type=jnp.float32
            )
            gated_ref[i * both : (i + 1) * both, :] = (sig_ref[i, columns, :] * attended).astype(
                jnp.bfloat16
            )
        mixed = jnp.dot(gated_ref[...], wo_ref[...], preferred_element_type=jnp.float32)
        mixed = mixed.reshape(rows, both, channels)
        for c in range(2):
            send_ref[first + c] = mixed[:, c * rows : (c + 1) * rows, :].astype(jnp.bfloat16)

    def out_copy(source, target):
        return pltpu.make_async_remote_copy(
            src_ref=send_ref.at[target],
            dst_ref=out_ref.at[pl.ds(pl.multiple_of(source * rows, rows), rows)],
            send_sem=out_send.at[target],
            recv_sem=out_recv.at[source],
            device_id={"row": target},
            device_id_type=MESH,
        )

    bias_copy(mate, mate, mate).wait_recv()
    attend(chip * 2)
    own = pltpu.make_async_copy(
        send_ref.at[me], out_ref.at[pl.ds(pl.multiple_of(me * rows, rows), rows)], own_sem
    )
    own.start()
    out_copy(me, mate).start()

    def one_chip(step, carry):
        peer = other(chip, step, chips) * 2
        for c in range(2):
            bias_copy(peer + c, peer + c, peer + c).wait_recv()
        attend(peer)
        for c in range(2):
            out_copy(me, peer + c).start()
        return carry

    lax.fori_loop(1, chips, one_chip, 0)

    def finish(peer):
        bias_copy(me, peer, peer).wait_send()
        out_copy(me, peer).wait_send()
        out_copy(peer, peer).wait_recv()

    finish(mate)

    def finish_chip(step, carry):
        peer = other(chip, step, chips) * 2
        for c in range(2):
            finish(peer + c)
        return carry

    lax.fori_loop(1, chips, finish_chip, 0)
    own.wait()


def local(
    n, pair_map, norm_gain, w_query, w_key, w_value, w_gate, w_bias, w_output, window_start, key_length
):
    rows, width, channels = pair_map.shape
    anywhere = pl.BlockSpec(memory_space=pl.ANY)
    scalars = pl.BlockSpec(memory_space=pltpu.SMEM)
    weight = pltpu.VMEM((channels, channels), jnp.bfloat16)
    return pl.pallas_call(
        functools.partial(kernel, n),
        out_shape=jax.ShapeDtypeStruct((n * rows, width // n, channels), jnp.bfloat16),
        in_specs=[anywhere] * 8 + [scalars] * 2,
        out_specs=anywhere,
        scratch_shapes=[
            pltpu.VMEM((rows, width, channels), jnp.bfloat16),
            pltpu.VMEM((1, channels), jnp.float32),
            weight,
            weight,
            weight,
            weight,
            pltpu.VMEM((channels, H), jnp.bfloat16),
            weight,
            pltpu.VMEM((channels, channels), jnp.float32),
            pltpu.VMEM((n, H, rows, width), jnp.float32),
            pltpu.VMEM((rows, width, H * width), jnp.float32),
            pltpu.VMEM((rows, H * width, channels), jnp.bfloat16),
            pltpu.VMEM((rows, width, channels), jnp.float32),
            pltpu.VMEM((2 * rows * rows, channels), jnp.bfloat16),
            pltpu.VMEM((n, rows, width // n, channels), jnp.bfloat16),
            pltpu.SemaphoreType.DMA((8,)),
            pltpu.SemaphoreType.DMA((n,)),
            pltpu.SemaphoreType.DMA((n,)),
            pltpu.SemaphoreType.DMA((n,)),
            pltpu.SemaphoreType.DMA((n,)),
            pltpu.SemaphoreType.DMA,
        ],
        compiler_params=pltpu.CompilerParams(
            collective_id=0, has_side_effects=True, vmem_limit_bytes=60 * 1024 * 1024
        ),
        name="attend",
    )(
        pair_map,
        norm_gain.reshape(1, channels),
        w_query,
        w_key,
        w_value,
        w_gate,
        w_bias,
        w_output,
        window_start,
        key_length,
    )


def solution(mesh):
    return jax.shard_map(
        functools.partial(local, mesh.shape["row"]),
        mesh=mesh,
        in_specs=(
            P(("grp", "row"), None, None),
            P(),
            P(),
            P(),
            P(),
            P(),
            P(),
            P(),
            P(("grp", "row")),
            P(("grp", "row")),
        ),
        out_specs=P("grp", "row", None),
        check_vma=False,
    )
```

```python
import functools
import math

import jax
import jax.numpy as jnp
from jax import lax
from jax.experimental import pallas as pl
from jax.experimental.pallas import tpu as pltpu
from jax.sharding import PartitionSpec as P

H = 4
LOG2E = math.log2(math.e)
MESH = pl.DeviceIdType.MESH
NT = (((1,), (1,)), ((), ()))


def other(index, step, count):
    if count & (count - 1):
        return lax.rem(index + step, count)
    result, bit = 0, 1
    while bit < count:
        a, b = index // bit % 2, step // bit % 2
        result = result + (a + b - 2 * a * b) * bit
        bit *= 2
    return result


def kernel(
    n,
    x_hbm,
    gain_hbm,
    wq_hbm,
    wk_hbm,
    wv_hbm,
    wg_hbm,
    wb_hbm,
    wo_hbm,
    start_ref,
    length_ref,
    out_ref,
    x_ref,
    gain_ref,
    wq_ref,
    wk_ref,
    wv_ref,
    wg_ref,
    wb_ref,
    wo_ref,
    bias_ref,
    score_ref,
    value_ref,
    sig_ref,
    gated_ref,
    send_ref,
    in_sem,
    bias_send,
    bias_recv,
    out_send,
    out_recv,
    own_sem,
):
    rows, width, channels = x_ref.shape
    head = channels // H
    chips = n // 2
    me = lax.axis_index("row")
    core, chip = me % 2, me // 2
    mate = me + 1 - 2 * core

    barrier = pltpu.get_barrier_semaphore()

    def greet(step, carry):
        pl.semaphore_signal(
            barrier, inc=1, device_id={"row": lax.rem(me + step, n)}, device_id_type=MESH
        )
        return carry

    lax.fori_loop(1, n, greet, 0)

    loads = [
        pltpu.make_async_copy(source, target, in_sem.at[at])
        for at, (source, target) in enumerate(
            (
                (x_hbm, x_ref),
                (gain_hbm, gain_ref),
                (wb_hbm, wb_ref),
                (wq_hbm, wq_ref),
                (wk_hbm, wk_ref),
                (wv_hbm, wv_ref),
                (wg_hbm, wg_ref),
                (wo_hbm, wo_ref),
            )
        )
    ]
    for load in loads:
        load.start()

    loads[2].wait()
    bias_weight = wb_ref[...]
    loads[0].wait()
    loads[1].wait()
    gain = gain_ref[...]
    normed = []
    for i in range(rows):
        values = x_ref[i].astype(jnp.float32)
        center = jnp.mean(values, axis=-1, keepdims=True)
        values = values - center
        spread = jnp.mean(values * values, axis=-1, keepdims=True)
        row = (values * lax.rsqrt(spread + 1e-05) * gain).astype(jnp.bfloat16)
        x_ref[i] = row
        local = lax.dot_general(bias_weight, row, NT, preferred_element_type=jnp.float32)
        local = local * LOG2E
        for h in range(H):
            bias_ref[me, h, i : i + 1, :] = local[h : h + 1]

    pl.semaphore_wait(barrier, n - 1)

    def bias_copy(source, target, slot):
        return pltpu.make_async_remote_copy(
            src_ref=bias_ref.at[source],
            dst_ref=bias_ref.at[source],
            send_sem=bias_send.at[slot],
            recv_sem=bias_recv.at[source],
            device_id={"row": target},
            device_id_type=MESH,
        )

    def send_bias(at, carry):
        peer = other(chip, chips - 1 - at, chips) * 2
        for c in range(2):
            bias_copy(me, peer + c, peer + c).start()
        return carry

    lax.fori_loop(0, chips - 1, send_bias, 0)
    bias_copy(me, mate, mate).start()

    for load in loads[3:7]:
        load.wait()
    lane = lax.broadcasted_iota(jnp.int32, (1, channels), 1) // head
    masks = [(lane == h).astype(jnp.float32).astype(jnp.bfloat16) for h in range(H)]
    place = lax.broadcasted_iota(jnp.int32, (1, width), 1)
    factor = LOG2E / head**0.5

    def project(i):
        row = x_ref[i]

        def through(weight):
            return jnp.dot(row, weight[...], preferred_element_type=jnp.float32)

        query = through(wq_ref).astype(jnp.bfloat16)
        key = through(wk_ref).astype(jnp.bfloat16)
        value = through(wv_ref).astype(jnp.bfloat16)
        gate = through(wg_ref).astype(jnp.bfloat16).astype(jnp.float32)
        sig_ref[i] = jax.nn.sigmoid(gate)
        first = start_ref[i]
        valid = (place >= first) & (place < first + length_ref[i])
        for h in range(H):
            span = slice(h * width, (h + 1) * width)
            value_ref[i, span, :] = value * masks[h]
            part = lax.dot_general(
                query, key * masks[h], NT, preferred_element_type=jnp.float32
            )
            score_ref[i, :, span] = jnp.where(valid, part * factor, jnp.float32(-1e30))

    if width <= 128:
        for i in range(rows):
            project(i)
    else:
        pl.loop(0, rows)(project)
    loads[7].wait()

    both = 2 * rows

    def attend(first):
        columns = pl.ds(pl.multiple_of(first * rows, both), both)
        biases = [bias_ref[pl.ds(first, 2), h].reshape(both, width) for h in range(H)]
        for i in range(rows):
            parts = []
            for h in range(H):
                t = score_ref[i, columns, h * width : (h + 1) * width] + biases[h]
                raised = jnp.exp2(t - jnp.max(t, axis=-1, keepdims=True))
                total = jnp.sum(raised, axis=-1, keepdims=True)
                parts.append((raised * (1.0 / total)).astype(jnp.bfloat16))
            attended = jnp.dot(
                jnp.concatenate(parts, axis=1), value_ref[i], preferred_element_type=jnp.float32
            )
            gated_ref[i * both : (i + 1) * both, :] = (sig_ref[i, columns, :] * attended).astype(
                jnp.bfloat16
            )
        mixed = jnp.dot(gated_ref[...], wo_ref[...], preferred_element_type=jnp.float32)
        mixed = mixed.reshape(rows, both, channels)
        for c in range(2):
            send_ref[first + c] = mixed[:, c * rows : (c + 1) * rows, :].astype(jnp.bfloat16)

    def out_copy(source, target):
        return pltpu.make_async_remote_copy(
            src_ref=send_ref.at[target],
            dst_ref=out_ref.at[pl.ds(pl.multiple_of(source * rows, rows), rows)],
            send_sem=out_send.at[target],
            recv_sem=out_recv.at[source],
            device_id={"row": target},
            device_id_type=MESH,
        )

    bias_copy(mate, mate, mate).wait_recv()
    attend(chip * 2)
    own = pltpu.make_async_copy(
        send_ref.at[me], out_ref.at[pl.ds(pl.multiple_of(me * rows, rows), rows)], own_sem
    )
    own.start()
    out_copy(me, mate).start()

    def one_chip(step, carry):
        peer = other(chip, step, chips) * 2
        for c in range(2):
            bias_copy(peer + c, peer + c, peer + c).wait_recv()
        attend(peer)
        for c in range(2):
            out_copy(me, peer + c).start()
        return carry

    lax.fori_loop(1, chips, one_chip, 0)

    def finish(peer):
        bias_copy(me, peer, peer).wait_send()
        out_copy(me, peer).wait_send()
        out_copy(peer, peer).wait_recv()

    finish(mate)

    def finish_chip(step, carry):
        peer = other(chip, step, chips) * 2
        for c in range(2):
            finish(peer + c)
        return carry

    lax.fori_loop(1, chips, finish_chip, 0)
    own.wait()


def local(
    n, pair_map, norm_gain, w_query, w_key, w_value, w_gate, w_bias, w_output, window_start, key_length
):
    rows, width, channels = pair_map.shape
    anywhere = pl.BlockSpec(memory_space=pl.ANY)
    outside = pl.BlockSpec(memory_space=pltpu.HBM)
    plane = rows * width * 4
    grant = 4 * 1024 * 1024 + plane * (2 * H * width + 2 * H * channels + 4 * channels)
    scalars = pl.BlockSpec(memory_space=pltpu.SMEM)
    weight = pltpu.VMEM((channels, channels), jnp.bfloat16)
    return pl.pallas_call(
        functools.partial(kernel, n),
        out_shape=pltpu.VMEM((n * rows, width // n, channels), jnp.bfloat16),
        in_specs=[outside] * 8 + [scalars] * 2,
        out_specs=pl.BlockSpec(memory_space=pltpu.VMEM),
        scratch_shapes=[
            pltpu.VMEM((rows, width, channels), jnp.bfloat16),
            pltpu.VMEM((1, channels), jnp.float32),
            weight,
            weight,
            weight,
            weight,
            pltpu.VMEM((H, channels), jnp.bfloat16),
            weight,
            pltpu.VMEM((n, H, rows, width), jnp.float32),
            pltpu.VMEM((rows, width, H * width), jnp.float32),
            pltpu.VMEM((rows, H * width, channels), jnp.bfloat16),
            pltpu.VMEM((rows, width, channels), jnp.float32),
            pltpu.VMEM((2 * rows * rows, channels), jnp.bfloat16),
            pltpu.VMEM((n, rows, width // n, channels), jnp.bfloat16),
            pltpu.SemaphoreType.DMA((8,)),
            pltpu.SemaphoreType.DMA((n,)),
            pltpu.SemaphoreType.DMA((n,)),
            pltpu.SemaphoreType.DMA((n,)),
            pltpu.SemaphoreType.DMA((n,)),
            pltpu.SemaphoreType.DMA,
        ],
        compiler_params=pltpu.CompilerParams(
            collective_id=0, has_side_effects=True, vmem_limit_bytes=56 * 1024 * 1024
        ),
        name="attend",
    )(
        pair_map,
        norm_gain.reshape(1, channels),
        w_query,
        w_key,
        w_value,
        w_gate,
        w_bias.T,
        w_output,
        window_start,
        key_length,
    )


def solution(mesh):
    return jax.shard_map(
        functools.partial(local, mesh.shape["row"]),
        mesh=mesh,
        in_specs=(
            P(("grp", "row"), None, None),
            P(),
            P(),
            P(),
            P(),
            P(),
            P(),
            P(),
            P(("grp", "row")),
            P(("grp", "row")),
        ),
        out_specs=P("grp", "row", None),
        check_vma=False,
    )
```

```python
import functools
import math

import jax
import jax.numpy as jnp
from jax import lax
from jax.experimental import pallas as pl
from jax.experimental.pallas import tpu as pltpu
from jax.sharding import PartitionSpec as P

H = 4
LOG2E = math.log2(math.e)
MESH = pl.DeviceIdType.MESH
NT = (((1,), (1,)), ((), ()))


def other(index, step, count):
    if count & (count - 1):
        return lax.rem(index + step, count)
    result, bit = 0, 1
    while bit < count:
        a, b = index // bit % 2, step // bit % 2
        result = result + (a + b - 2 * a * b) * bit
        bit *= 2
    return result


def kernel(
    n,
    x_hbm,
    gain_hbm,
    wq_hbm,
    wk_hbm,
    wv_hbm,
    wg_hbm,
    wb_hbm,
    wo_hbm,
    start_hbm,
    length_hbm,
    out_ref,
    x_ref,
    gain_ref,
    wq_ref,
    wk_ref,
    wv_ref,
    wg_ref,
    wb_ref,
    wo_ref,
    bias_ref,
    score_ref,
    key_ref,
    value_ref,
    sig_ref,
    gated_ref,
    send_ref,
    start_ref,
    length_ref,
    in_sem,
    bias_send,
    bias_recv,
    out_send,
    out_recv,
):
    rows, width, channels = x_ref.shape
    head = channels // H
    chips = n // 2
    me = lax.axis_index("row")
    core, chip = me % 2, me // 2
    mate = me + 1 - 2 * core

    barrier = pltpu.get_barrier_semaphore()

    def greet(at, carry):
        peer = other(chip, chips - 1 - at, chips) * 2
        for c in range(2):
            pl.semaphore_signal(barrier, inc=1, device_id={"row": peer + c}, device_id_type=MESH)
        return carry

    lax.fori_loop(0, chips - 1, greet, 0, unroll=chips <= 16)
    pl.semaphore_signal(barrier, inc=1, device_id={"row": mate}, device_id_type=MESH)

    def load(pairs, slot):
        copies = [pltpu.make_async_copy(source, target, in_sem.at[slot]) for source, target in pairs]
        for copy in copies:
            copy.start()
        return copies

    def arrived(copies):
        for copy in copies:
            copy.wait()

    first_in = load([(x_hbm, x_ref)], 0), load([(gain_hbm, gain_ref)], 1), load([(wb_hbm, wb_ref)], 2)
    weights_in = [
        load([pair], 3 + at)
        for at, pair in enumerate(
            (
                (wq_hbm, wq_ref),
                (wk_hbm, wk_ref),
                (wv_hbm, wv_ref),
                (wg_hbm, wg_ref),
                (wo_hbm, wo_ref),
                (start_hbm, start_ref),
                (length_hbm, length_ref),
            )
        )
    ]

    key_ref[...] = jnp.zeros_like(key_ref)
    for copies in first_in:
        arrived(copies)
    bias_weight = wb_ref[...]
    gain = gain_ref[...]
    normed = []
    for i in range(rows):
        values = x_ref[i].astype(jnp.float32)
        center = jnp.mean(values, axis=-1, keepdims=True)
        values = values - center
        spread = jnp.mean(values * values, axis=-1, keepdims=True)
        row = (values * lax.rsqrt(spread + 1e-05) * gain).astype(jnp.bfloat16)
        x_ref[i] = row
        local = lax.dot_general(bias_weight, row, NT, preferred_element_type=jnp.float32)
        local = local * LOG2E
        for h in range(H):
            bias_ref[me, h, i : i + 1, :] = local[h : h + 1]

    pl.semaphore_wait(barrier, n - 1)

    def bias_copy(source, target):
        return pltpu.make_async_remote_copy(
            src_ref=bias_ref.at[source],
            dst_ref=bias_ref.at[source],
            send_sem=bias_send,
            recv_sem=bias_recv.at[source],
            device_id={"row": target},
            device_id_type=MESH,
        )

    def send_bias(at, carry):
        bias_copy(me, other(chip, chips - 1 - at, chips) * 2 + core).start()
        return carry

    lax.fori_loop(0, chips - 1, send_bias, 0, unroll=chips <= 16)
    bias_copy(me, mate).start()

    def hand_over(step):
        source = other(chip, step, chips) * 2 + core
        bias_copy(source, mate).wait_recv()
        bias_copy(source, mate).start()

    for copies in weights_in:
        arrived(copies)
    lane = lax.broadcasted_iota(jnp.int32, (1, channels), 1) // head
    masks = [(lane == h).astype(jnp.float32).astype(jnp.bfloat16) for h in range(H)]
    place = lax.broadcasted_iota(jnp.int32, (1, width), 1)
    factor = LOG2E / head**0.5

    def project(i):
        row = x_ref[i]

        def through(weight):
            return jnp.dot(row, weight[...], preferred_element_type=jnp.float32)

        query = through(wq_ref).astype(jnp.bfloat16)
        key = through(wk_ref).astype(jnp.bfloat16)
        value = through(wv_ref).astype(jnp.bfloat16)
        gate = through(wg_ref).astype(jnp.bfloat16).astype(jnp.float32)
        sig_ref[i] = jax.nn.sigmoid(gate)
        first = start_ref[i]
        valid = (place >= first) & (place < first + length_ref[i])
        turned = key.T
        for h in range(H):
            span = slice(h * width, (h + 1) * width)
            part = slice(h * head, (h + 1) * head)
            value_ref[i, span, :] = value * masks[h]
            key_ref[i, part, span] = turned[part]
            scores = jnp.dot(query, key_ref[i, :, span], preferred_element_type=jnp.float32)
            score_ref[i, :, span] = jnp.where(valid, scores * factor, jnp.float32(-1e30))

    if width <= 128:
        for i in range(rows):
            project(i)
    else:
        pl.loop(0, rows)(project)

    both = 2 * rows

    def attend(first):
        columns = pl.ds(pl.multiple_of(first * rows, both), both)
        biases = [bias_ref[pl.ds(first, 2), h].reshape(both, width) for h in range(H)]
        for i in range(rows):
            parts = []
            for h in range(H):
                t = score_ref[i, columns, h * width : (h + 1) * width] + biases[h]
                raised = jnp.exp2(t - jnp.max(t, axis=-1, keepdims=True))
                total = jnp.sum(raised, axis=-1, keepdims=True)
                parts.append((raised * (1.0 / total)).astype(jnp.bfloat16))
            attended = jnp.dot(
                jnp.concatenate(parts, axis=1), value_ref[i], preferred_element_type=jnp.float32
            )
            gated_ref[i * both : (i + 1) * both, :] = (sig_ref[i, columns, :] * attended).astype(
                jnp.bfloat16
            )
        mixed = jnp.dot(gated_ref[...], wo_ref[...], preferred_element_type=jnp.float32)
        mixed = mixed.reshape(rows, both, channels)
        return mixed.astype(jnp.bfloat16)

    def out_copy(target):
        return pltpu.make_async_remote_copy(
            src_ref=send_ref.at[target],
            dst_ref=out_ref.at[pl.ds(pl.multiple_of(me * rows, rows), rows)],
            send_sem=out_send,
            recv_sem=out_recv,
            device_id={"row": target},
            device_id_type=MESH,
        )

    def send_chip(mixed, first, mine):
        for c in range(2):
            send_ref[first + c] = mixed[:, c * rows : (c + 1) * rows, :]
        if mine:
            out_ref[pl.ds(pl.multiple_of(me * rows, rows), rows)] = send_ref[me]
            out_copy(mate).start()
        else:
            for c in range(2):
                out_copy(first + c).start()

    def own_chip():
        bias_copy(mate, mate).wait_recv()
        send_chip(attend(chip * 2), chip * 2, True)

    def one_chip(step):
        peer = other(chip, step, chips) * 2
        bias_copy(peer + 1 - core, mate).wait_recv()
        send_chip(attend(peer), peer, False)

    if chips == 8:
        for step in (1, 2, 3):
            hand_over(step)
        own_chip()
        one_chip(1)
        for step in (4, 5):
            hand_over(step)
        one_chip(2)
        for step in (6, 7):
            hand_over(step)
        for step in (4, 5, 6, 7, 3):
            one_chip(step)
    else:
        hand_over(1)
        own_chip()

        def answer(step, carry):
            @pl.when(step < chips - 1)
            def _():
                hand_over(step + 1)

            one_chip(step)
            return carry

        lax.fori_loop(1, chips, answer, 0)

    rest = pltpu.make_async_remote_copy(
        src_ref=bias_ref.at[pl.ds(0, n - 1)],
        dst_ref=bias_ref.at[pl.ds(0, n - 1)],
        send_sem=bias_send,
        recv_sem=bias_recv.at[me],
        device_id={"row": mate},
        device_id_type=MESH,
    )
    rest.wait_send()
    rest = pltpu.make_async_remote_copy(
        src_ref=send_ref.at[pl.ds(0, n - 1)],
        dst_ref=out_ref.at[pl.ds(0, (n - 1) * rows)],
        send_sem=out_send,
        recv_sem=out_recv,
        device_id={"row": mate},
        device_id_type=MESH,
    )
    rest.wait_send()
    rest.wait_recv()


def local(
    n, pair_map, norm_gain, w_query, w_key, w_value, w_gate, w_bias, w_output, window_start, key_length
):
    rows, width, channels = pair_map.shape
    outside = pl.BlockSpec(memory_space=pltpu.HBM)
    weight = pltpu.VMEM((channels, channels), jnp.bfloat16)
    return pl.pallas_call(
        functools.partial(kernel, n),
        out_shape=pltpu.VMEM((n * rows, width // n, channels), jnp.bfloat16),
        in_specs=[outside] * 10,
        out_specs=pl.BlockSpec(memory_space=pltpu.VMEM),
        scratch_shapes=[
            pltpu.VMEM((rows, width, channels), jnp.bfloat16),
            pltpu.VMEM((1, channels), jnp.float32),
            weight,
            weight,
            weight,
            weight,
            pltpu.VMEM((H, channels), jnp.bfloat16),
            weight,
            pltpu.VMEM((n, H, rows, width), jnp.float32),
            pltpu.VMEM((rows, width, H * width), jnp.float32),
            pltpu.VMEM((rows, channels, H * width), jnp.bfloat16),
            pltpu.VMEM((rows, H * width, channels), jnp.bfloat16),
            pltpu.VMEM((rows, width, channels), jnp.float32),
            pltpu.VMEM((2 * rows * rows, channels), jnp.bfloat16),
            pltpu.VMEM((n, rows, width // n, channels), jnp.bfloat16),
            pltpu.SMEM((rows,), jnp.int32),
            pltpu.SMEM((rows,), jnp.int32),
            pltpu.SemaphoreType.DMA((10,)),
            pltpu.SemaphoreType.DMA,
            pltpu.SemaphoreType.DMA((n,)),
            pltpu.SemaphoreType.DMA,
            pltpu.SemaphoreType.DMA,
        ],
        compiler_params=pltpu.CompilerParams(
            collective_id=0, has_side_effects=True, vmem_limit_bytes=56 * 1024 * 1024
        ),
        name="attend",
    )(
        pair_map,
        norm_gain.reshape(1, channels),
        w_query,
        w_key,
        w_value,
        w_gate,
        w_bias.T,
        w_output,
        window_start,
        key_length,
    )


def solution(mesh):
    return jax.shard_map(
        functools.partial(local, mesh.shape["row"]),
        mesh=mesh,
        in_specs=(
            P(("grp", "row"), None, None),
            P(),
            P(),
            P(),
            P(),
            P(),
            P(),
            P(),
            P(("grp", "row")),
            P(("grp", "row")),
        ),
        out_specs=P("grp", "row", None),
        check_vma=False,
    )
```

```python
import functools
import math

import jax
import jax.numpy as jnp
from jax import lax
from jax.experimental import pallas as pl
from jax.experimental.pallas import tpu as pltpu
from jax.sharding import PartitionSpec as P

H = 4
LOG2E = math.log2(math.e)
MESH = pl.DeviceIdType.MESH
NT = (((1,), (1,)), ((), ()))


def other(index, step, count):
    if count & (count - 1):
        return lax.rem(index + step, count)
    result, bit = 0, 1
    while bit < count:
        a, b = index // bit % 2, step // bit % 2
        result = result + (a + b - 2 * a * b) * bit
        bit *= 2
    return result


def kernel(
    n,
    x_hbm,
    gain_hbm,
    wq_hbm,
    wk_hbm,
    wv_hbm,
    wg_hbm,
    wb_hbm,
    wo_hbm,
    start_hbm,
    length_hbm,
    out_ref,
    x_ref,
    gain_ref,
    wq_ref,
    wk_ref,
    wv_ref,
    wg_ref,
    wb_ref,
    wo_ref,
    bias_ref,
    score_ref,
    value_ref,
    sig_ref,
    gated_ref,
    send_ref,
    start_ref,
    length_ref,
    in_sem,
    bias_send,
    bias_recv,
    out_send,
    out_recv,
):
    rows, width, channels = x_ref.shape
    head = channels // H
    chips = n // 2
    me = lax.axis_index("row")
    core, chip = me % 2, me // 2
    mate = me + 1 - 2 * core

    def load(pairs, slot):
        copies = [pltpu.make_async_copy(source, target, in_sem.at[slot]) for source, target in pairs]
        for copy in copies:
            copy.start()
        return copies

    def arrived(copies):
        for copy in copies:
            copy.wait()

    first_in = load([(x_hbm, x_ref)], 0), load([(gain_hbm, gain_ref)], 1), load([(wb_hbm, wb_ref)], 2)
    barrier = pltpu.get_barrier_semaphore()

    def greet(at, carry):
        peer = other(chip, chips - 1 - at, chips) * 2
        for c in range(2):
            pl.semaphore_signal(barrier, inc=1, device_id={"row": peer + c}, device_id_type=MESH)
        return carry

    lax.fori_loop(0, chips - 1, greet, 0, unroll=chips <= 16)
    pl.semaphore_signal(barrier, inc=1, device_id={"row": mate}, device_id_type=MESH)

    weights_in = [
        load([pair], 3 + at)
        for at, pair in enumerate(
            (
                (wq_hbm, wq_ref),
                (wk_hbm, wk_ref),
                (wv_hbm, wv_ref),
                (wg_hbm, wg_ref),
                (wo_hbm, wo_ref),
                (start_hbm, start_ref),
                (length_hbm, length_ref),
            )
        )
    ]

    for copies in first_in:
        arrived(copies)
    bias_weight = wb_ref[...]
    gain = gain_ref[...]
    ones = jnp.ones((channels, channels), jnp.bfloat16)
    for i in range(rows):
        row = x_ref[i]
        center = jnp.dot(row, ones, preferred_element_type=jnp.float32) * (1.0 / channels)
        values = row.astype(jnp.float32) - center
        spread = jnp.mean(values * values, axis=-1, keepdims=True)
        row = (values * lax.rsqrt(spread + 1e-05) * gain).astype(jnp.bfloat16)
        x_ref[i] = row
        local = lax.dot_general(bias_weight, row, NT, preferred_element_type=jnp.float32)
        local = local * LOG2E
        for h in range(H):
            bias_ref[me, h, i : i + 1, :] = local[h : h + 1]

    pl.semaphore_wait(barrier, n - 1)

    def bias_copy(source, target):
        return pltpu.make_async_remote_copy(
            src_ref=bias_ref.at[source],
            dst_ref=bias_ref.at[source],
            send_sem=bias_send,
            recv_sem=bias_recv.at[source],
            device_id={"row": target},
            device_id_type=MESH,
        )

    near = chips // 2

    def send_far(at, carry):
        bias_copy(me, other(chip, chips - 1 - at, chips) * 2 + core).start()
        return carry

    def send_near(at, carry):
        peer = other(chip, near - 1 - at, chips) * 2
        bias_copy(me, peer).start()
        bias_copy(me, peer + 1).start()
        return carry

    lax.fori_loop(0, chips - near, send_far, 0, unroll=chips <= 16)
    lax.fori_loop(0, near - 1, send_near, 0, unroll=chips <= 16)
    bias_copy(me, mate).start()

    def hand_over(step):
        source = other(chip, step, chips) * 2 + core
        bias_copy(source, mate).wait_recv()
        bias_copy(source, mate).start()

    for copies in weights_in:
        arrived(copies)
    lane = lax.broadcasted_iota(jnp.int32, (1, channels), 1) // head
    masks = [(lane == h).astype(jnp.float32).astype(jnp.bfloat16) for h in range(H)]
    place = lax.broadcasted_iota(jnp.int32, (1, width), 1)
    factor = LOG2E / head**0.5

    def project(i):
        row = x_ref[i]

        def through(weight):
            return jnp.dot(row, weight[...], preferred_element_type=jnp.float32)

        query = through(wq_ref).astype(jnp.bfloat16)
        key = through(wk_ref).astype(jnp.bfloat16)
        value = through(wv_ref).astype(jnp.bfloat16)
        gate = through(wg_ref).astype(jnp.bfloat16).astype(jnp.float32)
        sig_ref[i] = jax.nn.sigmoid(gate)
        first = start_ref[i]
        valid = (place >= first) & (place < first + length_ref[i])
        for h in range(H):
            span = slice(h * width, (h + 1) * width)
            value_ref[i, span, :] = value * masks[h]
            part = lax.dot_general(
                query, key * masks[h], NT, preferred_element_type=jnp.float32
            )
            score_ref[i, :, span] = jnp.where(valid, part * factor, jnp.float32(-1e30))

    if width <= 128:
        for i in range(rows):
            project(i)
    else:
        pl.loop(0, rows)(project)

    both = 2 * rows

    def attend(first):
        columns = pl.ds(pl.multiple_of(first * rows, both), both)
        biases = [bias_ref[pl.ds(first, 2), h].reshape(both, width) for h in range(H)]
        for i in range(rows):
            parts = []
            for h in range(H):
                t = score_ref[i, columns, h * width : (h + 1) * width] + biases[h]
                raised = jnp.exp2(t - jnp.max(t, axis=-1, keepdims=True))
                total = jnp.sum(raised, axis=-1, keepdims=True)
                parts.append((raised * (1.0 / total)).astype(jnp.bfloat16))
            attended = jnp.dot(
                jnp.concatenate(parts, axis=1), value_ref[i], preferred_element_type=jnp.float32
            )
            gated_ref[i * both : (i + 1) * both, :] = (sig_ref[i, columns, :] * attended).astype(
                jnp.bfloat16
            )
        mixed = jnp.dot(gated_ref[...], wo_ref[...], preferred_element_type=jnp.float32)
        mixed = mixed.reshape(rows, both, channels)
        return mixed.astype(jnp.bfloat16)

    def out_copy(target):
        return pltpu.make_async_remote_copy(
            src_ref=send_ref.at[target],
            dst_ref=out_ref.at[pl.ds(pl.multiple_of(me * rows, rows), rows)],
            send_sem=out_send,
            recv_sem=out_recv,
            device_id={"row": target},
            device_id_type=MESH,
        )

    def send_chip(mixed, first, mine):
        for c in range(2):
            send_ref[first + c] = mixed[:, c * rows : (c + 1) * rows, :]
        if mine:
            out_ref[pl.ds(pl.multiple_of(me * rows, rows), rows)] = send_ref[me]
            out_copy(mate).start()
        else:
            for c in range(2):
                out_copy(first + c).start()

    def one_chip(step):
        peer = other(chip, step, chips) * 2
        for c in range(2):
            bias_copy(peer + c, mate).wait_recv()
        send_chip(attend(peer), peer, False)

    def far_chip(step):
        peer = other(chip, step, chips) * 2
        bias_copy(peer + 1 - core, mate).wait_recv()
        send_chip(attend(peer), peer, False)

    bias_copy(mate, mate).wait_recv()
    send_chip(attend(chip * 2), chip * 2, True)
    if chips <= 8:
        for step in range(1, near - 1):
            one_chip(step)
        hand_over(near)
        one_chip(near - 1)
        for step in range(near + 1, chips):
            hand_over(step)
            far_chip(step - 1)
    else:
        pl.loop(1, near - 1)(one_chip)
        hand_over(near)
        one_chip(near - 1)

        @pl.loop(near + 1, chips)
        def _(step):
            hand_over(step)
            far_chip(step - 1)

    far_chip(chips - 1)

    rest = pltpu.make_async_remote_copy(
        src_ref=bias_ref.at[pl.ds(0, n - 1)],
        dst_ref=bias_ref.at[pl.ds(0, n - 1)],
        send_sem=bias_send,
        recv_sem=bias_recv.at[me],
        device_id={"row": mate},
        device_id_type=MESH,
    )
    rest.wait_send()
    rest = pltpu.make_async_remote_copy(
        src_ref=send_ref.at[pl.ds(0, n - 1)],
        dst_ref=out_ref.at[pl.ds(0, (n - 1) * rows)],
        send_sem=out_send,
        recv_sem=out_recv,
        device_id={"row": mate},
        device_id_type=MESH,
    )
    rest.wait_send()
    rest.wait_recv()


def local(
    n, pair_map, norm_gain, w_query, w_key, w_value, w_gate, w_bias, w_output, window_start, key_length
):
    rows, width, channels = pair_map.shape
    outside = pl.BlockSpec(memory_space=pltpu.HBM)
    weight = pltpu.VMEM((channels, channels), jnp.bfloat16)
    return pl.pallas_call(
        functools.partial(kernel, n),
        out_shape=pltpu.VMEM((n * rows, width // n, channels), jnp.bfloat16),
        in_specs=[outside] * 10,
        out_specs=pl.BlockSpec(memory_space=pltpu.VMEM),
        scratch_shapes=[
            pltpu.VMEM((rows, width, channels), jnp.bfloat16),
            pltpu.VMEM((1, channels), jnp.float32),
            weight,
            weight,
            weight,
            weight,
            pltpu.VMEM((H, channels), jnp.bfloat16),
            weight,
            pltpu.VMEM((n, H, rows, width), jnp.float32),
            pltpu.VMEM((rows, width, H * width), jnp.float32),
            pltpu.VMEM((rows, H * width, channels), jnp.bfloat16),
            pltpu.VMEM((rows, width, channels), jnp.float32),
            pltpu.VMEM((2 * rows * rows, channels), jnp.bfloat16),
            pltpu.VMEM((n, rows, width // n, channels), jnp.bfloat16),
            pltpu.SMEM((rows,), jnp.int32),
            pltpu.SMEM((rows,), jnp.int32),
            pltpu.SemaphoreType.DMA((10,)),
            pltpu.SemaphoreType.DMA,
            pltpu.SemaphoreType.DMA((n,)),
            pltpu.SemaphoreType.DMA,
            pltpu.SemaphoreType.DMA,
        ],
        compiler_params=pltpu.CompilerParams(
            collective_id=0, has_side_effects=True, vmem_limit_bytes=56 * 1024 * 1024
        ),
        name="attend",
    )(
        pair_map,
        norm_gain.reshape(1, channels),
        w_query,
        w_key,
        w_value,
        w_gate,
        w_bias.T,
        w_output,
        window_start,
        key_length,
    )


def solution(mesh):
    return jax.shard_map(
        functools.partial(local, mesh.shape["row"]),
        mesh=mesh,
        in_specs=(
            P(("grp", "row"), None, None),
            P(),
            P(),
            P(),
            P(),
            P(),
            P(),
            P(),
            P(("grp", "row")),
            P(("grp", "row")),
        ),
        out_specs=P("grp", "row", None),
        check_vma=False,
    )
```
